512 devices in a mesh: row: 32 (over x, y), col: 16 (over z, core).
Axes of the slice: x: 4, y: 8, z: 8, core: 2. Of those that a mesh axis runs over, the one named last changes fastest.
Arguments:
- parent_sigma: float32 [4, 32, 128, 8, 16, 128], P(None, 'row', None, None, 'col'), as said below
- slot_tile: int32 [32, 2], replicated, may hold values from 0 to 3, as said below
- slot_count: int32 [32], replicated, may hold values from 1 to 2, as said below
- panel: float32 [32, 2, 128, 1024], P('row'), may hold values from -0.25 to 0.25
- sep_factor: float32 [1024, 1024], P('row'), as said below
Outputs:
- sigma_update: float32 [32, 2, 128, 1024], P('row')
- sigma_sep: float32 [1024, 1024], P('row')
The draws below stay inside these ranges and needn't reach their ends.
Inputs may be any that keep to these rules, and one draw needn't show every extreme that they name: `parent_sigma`: symmetric when viewed as a [16384, 16384] matrix. `slot_tile`: the slots of one grid row name distinct tiles in increasing order. `slot_count`: every grid row has a live slot; some grid row has all 2 slots live. `sep_factor`: lower triangular with diagonal entries from 1.5 to 3.
All inputs are finite; a program needn't handle non-finite values.
Results may differ from the reference program's by a relative error of at most 0.00024.
Values sent between devices are 32-bit elements; how exact they have to be, the bound alone decides.
No kernel may reach another device: no remote copies, remote signals or barrier semaphores. Data moves between devices by JAX's collectives and lax.ppermute only.
A program may use at most 64 MiB of HBM per device.

```python
import math
import jax
import jax.numpy as jnp
from jax import lax

TB = 128
NB = 512
UCAP = 2
PPT = 4
PQT = 8
PAR = 16384
NS = 8192
SEP = 1024
N_ROW = 32
N_COL = 16


def draw_parent_sigma(key, part):
    base_key = jax.random.fold_in(key, 5)
    square = jax.random.normal(base_key, (PAR, PAR), jnp.float32)
    balanced = (square + square.T) * (0.5 / math.sqrt(2.0))
    clipped = jnp.clip(balanced, -3.0, 3.0)
    return clipped.reshape(PPT, N_ROW, TB, PQT, N_COL, TB).astype(jnp.float32)


def draw_slot_tile(key, part):
    base_key = jax.random.fold_in(key, 11)
    row_keys = jax.random.split(base_key, N_ROW)

    def one_row(row_key):
        return jnp.sort(jax.random.permutation(row_key, PPT)[:UCAP]).astype(jnp.int32)
    return jax.vmap(one_row)(row_keys)


def draw_slot_count(key, part):
    base_key = jax.random.fold_in(key, 23)
    count_key, full_key = jax.random.split(base_key)
    counts = jax.random.randint(count_key, (N_ROW,), 1, UCAP + 1)
    full_row = jax.random.randint(full_key, (), 0, N_ROW)
    return jnp.where(jnp.arange(N_ROW) == full_row, UCAP, counts).astype(jnp.int32)


def draw_sep_factor(key, part):
    base_key = jax.random.fold_in(key, 37)
    diag_key, chain_key, sign_key, far_key = jax.random.split(base_key, 4)
    row_index = jnp.arange(SEP)[:, None]
    col_index = jnp.arange(SEP)[None, :]
    diagonal = jax.random.uniform(diag_key, (SEP, 1), jnp.float32, 1.5, 3.0)
    ratio = jax.random.uniform(chain_key, (SEP, 1), jnp.float32, 0.6, 0.85)
    signs = jnp.where(jax.random.bernoulli(sign_key, 0.5, (SEP, 1)), 1.0, -1.0).astype(jnp.float32)
    far_part = jax.random.normal(far_key, (SEP, SEP), jnp.float32) / math.sqrt(NB)
    same_block = row_index // NB == col_index // NB
    next_below = row_index == col_index + 1
    inside = jnp.where(next_below, signs * ratio * diagonal, far_part)
    below = jnp.where(same_block, inside, far_part)
    return jnp.where(row_index > col_index, below, jnp.where(row_index == col_index, diagonal, 0.0)).astype(jnp.float32)


def level_of(rng, shape, cuts, smallest, high):
    loudness, own = 1.0, jax.random.fold_in(rng, 6)
    for position, blocks in cuts:
        draws = jnp.exp(jax.random.uniform(jax.random.fold_in(own, position), (blocks,), jnp.float32, smallest / len(cuts), high / len(cuts)))
        loudness = loudness * jnp.repeat(draws, shape[position] // blocks).reshape([-1 if axis == position else 1 for axis in range(len(shape))])
    return loudness


def gaussian(stream_key, dims, deviation, limit, pieces=(), held_as=jnp.bfloat16):
    result = deviation * jax.random.normal(stream_key, dims, jnp.float32)
    if pieces:
        result = result * level_of(stream_key, dims, pieces, -0.22, 0.18)
    return jnp.clip(result, -limit, limit).astype(held_as)


def setup_inputs(seed: int = 0) -> dict:
    key_list = jax.random.split(jax.random.key(seed), 6)
    return {
        "parent_sigma": draw_parent_sigma(jax.random.fold_in(key_list[5], 71), 0),
        "slot_tile": draw_slot_tile(jax.random.fold_in(key_list[5], 71), 0),
        "slot_count": draw_slot_count(jax.random.fold_in(key_list[5], 71), 0),
        "panel": gaussian(key_list[3], (N_ROW, UCAP, TB, SEP), NB ** -0.5, 0.25, ((0, 32),), jnp.float32),
        "sep_factor": draw_sep_factor(jax.random.fold_in(key_list[5], 71), 0),
    }


def exact_dot(left, right):
    return jnp.dot(left.astype(jnp.float32), right.astype(jnp.float32), precision=lax.Precision.HIGHEST, preferred_element_type=jnp.float32)

def lower_inverse(triangle):
    identity = jnp.eye(triangle.shape[0], dtype=jnp.float32)
    return jax.scipy.linalg.solve_triangular(triangle, identity, lower=True)

def reference(parent_sigma, slot_tile, slot_count, panel, sep_factor):
    owners = jnp.arange(N_ROW, dtype=jnp.int32)[:, None]
    parent_tiles = (slot_tile * N_ROW + owners).astype(jnp.int32)
    offsets = jnp.arange(TB, dtype=jnp.int32)
    update_rows = (parent_tiles[:, :, None] * TB + offsets[None, None, :]).reshape(-1).astype(jnp.int32)
    live_slots = jnp.arange(UCAP, dtype=jnp.int32)[None, :] < slot_count[:, None]
    live_rows = jnp.broadcast_to(live_slots[:, :, None], (N_ROW, UCAP, TB)).reshape(-1, 1).astype(jnp.float32)
    whole_sigma = parent_sigma.reshape(PAR, PAR)
    sigma_inner = jnp.take(jnp.take(whole_sigma, update_rows, axis=0), update_rows, axis=1)
    strips = panel.reshape(NS, SEP) * live_rows
    first_inv = lower_inverse(sep_factor[:NB, :NB])
    last_inv = lower_inverse(sep_factor[NB:, NB:])
    coupling = exact_dot(sep_factor[NB:, :NB], first_inv)
    last_u = exact_dot(strips[:, NB:], last_inv)
    first_u = exact_dot(strips[:, :NB], first_inv)
    last_y = exact_dot(sigma_inner, last_u)
    sigma_last = exact_dot(last_inv.T, last_inv) + exact_dot(last_u.T, last_y)
    first_y = exact_dot(sigma_inner, first_u) - exact_dot(last_y, coupling)
    sigma_cross = exact_dot(sigma_last, coupling) - exact_dot(last_y.T, first_u)
    sigma_first = exact_dot(first_inv.T, first_inv) + exact_dot(first_u.T, first_y) + exact_dot(coupling.T, sigma_cross)
    sigma_update = (-jnp.concatenate([first_y, last_y], axis=1) * live_rows).reshape(N_ROW, UCAP, TB, SEP)
    upper_rows = jnp.concatenate([sigma_first, -sigma_cross.T], axis=1)
    lower_rows = jnp.concatenate([-sigma_cross, sigma_last], axis=1)
    return (sigma_update, jnp.concatenate([upper_rows, lower_rows], axis=0))
```

```python
import functools

import jax
import jax.numpy as jnp
import numpy as np
from jax import lax
from jax.experimental import pallas as pl
from jax.experimental.pallas import tpu as pltpu
from jax.sharding import Mesh
from jax.sharding import PartitionSpec as P

ROW = ("x", "y")
COL = ("z", "core")
X, Y, Z, CORE = 4, 8, 8, 2
N_ROW, N_COL = X * Y, Z * CORE
TILE = 128
SEP = 1024
STRIPE = SEP // X
PACKED = STRIPE * X * (X + 1) // 2
WIDTH = SEP // N_COL
OWN = SEP // N_ROW
LINES = OWN // N_COL
MIB = 1024 * 1024
HIGHEST = lax.Precision.HIGHEST


def exact_dot(left, right):
    return jnp.dot(left, right, precision=HIGHEST, preferred_element_type=jnp.float32)


def front_kernel(tile_ref, count_ref, me_ref, upper_ref, lower_ref, panel_ref, out_ref):
    row, col = me_ref[0], me_ref[1]
    live = [(slot < count_ref[row]).astype(jnp.float32) for slot in range(2)]
    strips = jnp.concatenate([panel_ref[0, slot] * live[slot] for slot in range(2)], axis=0)
    strips_t = strips.T
    for step in range(2):
        owner = col + N_COL * step
        block = jnp.concatenate(
            [
                jnp.concatenate(
                    [sigma[0, pl.ds(tile_ref[owner, slot] * 2 + step, TILE, stride=8), :] for slot in range(2)],
                    axis=1,
                )
                for sigma in (upper_ref, lower_ref)
            ],
            axis=0,
        )
        out_ref[step] = exact_dot(strips_t, block)


def front(slot_tile, slot_count, me, sigma, panel):
    def slab(slot):
        return pl.BlockSpec((1, TILE * 8, TILE), lambda i, tile, count, me: (tile[me[0], slot], 0, 0))

    return pl.pallas_call(
        front_kernel,
        grid_spec=pltpu.PrefetchScalarGridSpec(
            num_scalar_prefetch=3,
            grid=(1,),
            in_specs=[
                slab(0),
                slab(1),
                pl.BlockSpec((1, 2, TILE, SEP), lambda i, *_: (0, 0, 0, 0)),
            ],
            out_specs=pl.BlockSpec((2, SEP, 2 * TILE), lambda i, *_: (0, 0, 0)),
        ),
        out_shape=pltpu.VMEM((2, SEP, 2 * TILE), jnp.float32),
        compiler_params=pltpu.CompilerParams(vmem_limit_bytes=16 * MIB),
        name="front",
    )(slot_tile, slot_count, me, sigma, sigma, panel)


def invert_tiles(tiles):
    row = lax.broadcasted_iota(jnp.int32, (TILE, TILE), 0)
    col = lax.broadcasted_iota(jnp.int32, (TILE, TILE), 1)

    def left_of(size):
        return (row // (2 * size) == col // (2 * size)) & (row // size > col // size)

    inverses = []
    for tile in tiles:
        scale = jnp.where(row == col, 1.0 / jnp.where(row == col, tile, 1.0), 0.0)
        down = jnp.sum(scale, axis=1, keepdims=True)
        across = jnp.sum(scale, axis=0, keepdims=True)
        inverses.append(scale - jnp.where(left_of(1), tile * down * across, 0.0))
    size = 2
    while size < TILE:
        mask = left_of(size)
        products = [exact_dot(jnp.where(mask, tile, 0.0), inverse) for tile, inverse in zip(tiles, inverses)]
        inverses = [inverse - exact_dot(inverse, product) for inverse, product in zip(inverses, products)]
        size *= 2
    return inverses


def inverse_kernel(share_ref, out_ref, packed_ref):
    for block in range(PACKED // TILE):
        for y in range(Y):
            for line in range(LINES):
                start = (block * Y + y) * LINES + line
                taken = share_ref[pl.ds(start, N_COL, stride=PACKED // TILE * Y * LINES), :]
                packed_ref[block, pl.ds(y * OWN + line, N_COL, stride=LINES), :] = taken

    def factor(stripe, start, width):
        first = (STRIPE * stripe * (stripe + 1) // 2 + start) // TILE
        return jnp.concatenate([packed_ref[first + block] for block in range(width // TILE)], axis=1)

    diagonals = [factor(stripe, stripe * STRIPE, STRIPE) for stripe in range(X)]
    tiles = [d[p * TILE : (p + 1) * TILE, p * TILE : (p + 1) * TILE] for d in diagonals for p in range(2)]
    inverses = invert_tiles(tiles)
    middles = [exact_dot(d[TILE:, :TILE], inverses[2 * stripe]) for stripe, d in enumerate(diagonals)]
    corners = [-exact_dot(inverses[2 * stripe + 1], middle) for stripe, middle in enumerate(middles)]
    for stripe in range(X):
        top = stripe * STRIPE
        out_ref[top : top + TILE, top : top + TILE] = inverses[2 * stripe]
        out_ref[top : top + TILE, top + TILE :] = jnp.zeros((TILE, SEP - top - TILE), jnp.float32)
        out_ref[top + TILE : top + STRIPE, top : top + TILE] = corners[stripe]
        out_ref[top + TILE : top + STRIPE, top + TILE : top + STRIPE] = inverses[2 * stripe + 1]
        if stripe < X - 1:
            out_ref[top + TILE : top + STRIPE, top + STRIPE :] = jnp.zeros((TILE, SEP - top - STRIPE), jnp.float32)
    products = []
    for stripe in (1, 3):
        left = (stripe - 1) * STRIPE
        above = out_ref[left : left + STRIPE, left : left + STRIPE]
        products.append(exact_dot(factor(stripe, left, STRIPE), above))
    for stripe, product in zip((1, 3), products):
        top = stripe * STRIPE
        own = out_ref[top : top + STRIPE, top : top + STRIPE]
        out_ref[top : top + STRIPE, top - STRIPE : top] = -exact_dot(own, product)
    half = 2 * STRIPE
    left_part = jnp.concatenate([factor(2, 0, half), factor(3, 0, half)], axis=0)
    first_cols = exact_dot(left_part, out_ref[:half, :STRIPE])
    last_cols = exact_dot(left_part[:, STRIPE:], out_ref[STRIPE:half, STRIPE:half])
    product = jnp.concatenate([first_cols, last_cols], axis=1)
    out_ref[half : half + STRIPE, :half] = -exact_dot(out_ref[half : half + STRIPE, half : half + STRIPE], product[:STRIPE])
    out_ref[half + STRIPE :, :half] = -exact_dot(out_ref[half + STRIPE :, half:], product)


VMEM = pl.BlockSpec(memory_space=pltpu.VMEM)
SMEM = pl.BlockSpec(memory_space=pltpu.SMEM)


def on_chip(value):
    return pltpu.with_memory_space_constraint(value, pltpu.VMEM)


def factor_inverse(shares):
    return pl.pallas_call(
        inverse_kernel,
        in_specs=[VMEM],
        out_specs=VMEM,
        out_shape=pltpu.VMEM((SEP, SEP), jnp.float32),
        scratch_shapes=[pltpu.VMEM((PACKED // TILE, STRIPE, TILE), jnp.float32)],
        compiler_params=pltpu.CompilerParams(vmem_limit_bytes=20 * MIB),
        name="factor_inverse",
    )(shares)


def times_inverse(left, inverse_ref, stripe):
    start = stripe * STRIPE
    return exact_dot(left[:, start:], inverse_ref[start:, start : start + STRIPE])


def separator_kernel(me_ref, count_ref, piece_ref, panel_ref, inverse_ref, out_ref):
    row, col = me_ref[0], me_ref[1]
    live = [(slot < count_ref[row]).astype(jnp.float32) for slot in range(2)]
    strips = jnp.concatenate([panel_ref[0, slot] * live[slot] for slot in range(2)], axis=0)
    local = exact_dot(piece_ref[...], strips)
    down = lax.broadcasted_iota(jnp.int32, (WIDTH, SEP), 0) + col * WIDTH
    across = lax.broadcasted_iota(jnp.int32, (WIDTH, SEP), 1)
    local = local + jnp.where((down == across) & (row == 0), 1.0, 0.0)
    for stripe in range(X):
        turned = times_inverse(local, inverse_ref, stripe).T
        for place in range(STRIPE // OWN):
            start = place * OWN
            out_ref[stripe * (STRIPE // OWN) + place] = jnp.concatenate(
                [turned[start : start + OWN // 2], turned[start + OWN // 2 : start + OWN]], axis=1
            )


def separator(me, slot_count, piece, panel, inverse):
    return pl.pallas_call(
        separator_kernel,
        in_specs=[SMEM, SMEM, VMEM, VMEM, VMEM],
        out_specs=VMEM,
        out_shape=jax.ShapeDtypeStruct((N_ROW, OWN // 2, 2 * WIDTH), jnp.float32),
        compiler_params=pltpu.CompilerParams(vmem_limit_bytes=14 * MIB),
        name="separator",
    )(me, slot_count, piece, panel, on_chip(inverse))


def final_kernel(me_ref, count_ref, whole_ref, blocks_ref, inverse_ref, update_ref, sep_ref):
    row = me_ref[0]
    turned = whole_ref[...].T
    parts = [turned[slot * TILE : (slot + 1) * TILE] * -(slot < count_ref[row]).astype(jnp.float32) for slot in range(2)]
    for side in range(2):
        lanes = slice(side * WIDTH, (side + 1) * WIDTH)
        parts.append(jnp.concatenate([blocks_ref[place][:, lanes] for place in range(N_COL)], axis=1))
    left = jnp.concatenate(parts, axis=0)
    for stripe in range(X):
        lanes = slice(stripe * STRIPE, (stripe + 1) * STRIPE)
        result = times_inverse(left, inverse_ref, stripe)
        update_ref[0, 0, :, lanes] = result[:TILE]
        update_ref[0, 1, :, lanes] = result[TILE : 2 * TILE]
        sep_ref[:, lanes] = result[2 * TILE :]


def final(me, slot_count, whole, blocks, inverse):
    return pl.pallas_call(
        final_kernel,
        in_specs=[SMEM, SMEM, VMEM, VMEM, VMEM],
        out_specs=(VMEM, VMEM),
        out_shape=(
            jax.ShapeDtypeStruct((1, 2, TILE, SEP), jnp.float32),
            jax.ShapeDtypeStruct((OWN, SEP), jnp.float32),
        ),
        compiler_params=pltpu.CompilerParams(vmem_limit_bytes=14 * MIB),
        name="final",
    )(me, slot_count, whole, blocks, on_chip(inverse))


def total_kernel(pieces_ref, out_ref):
    out_ref[...] = jnp.sum(pieces_ref[...], axis=0)


def total(pieces):
    return pl.pallas_call(
        total_kernel,
        in_specs=[VMEM],
        out_specs=VMEM,
        out_shape=jax.ShapeDtypeStruct(pieces.shape[1:], jnp.float32),
        compiler_params=pltpu.CompilerParams(vmem_limit_bytes=8 * MIB),
        name="total",
    )(on_chip(pieces))


def spread(value, size):
    return jnp.broadcast_to(value[None], (size, *value.shape))


def exchange(blocks, axis):
    return lax.all_to_all(blocks, axis, 0, 0, tiled=True)


def spread_lines(sep_factor, col):
    return exchange(spread(lax.dynamic_slice_in_dim(sep_factor, col * LINES, LINES, 0), N_ROW), ROW)


def gather_factor(lines):
    stripes = lines.reshape(X, Y * LINES, SEP // TILE, TILE)
    count = STRIPE // TILE
    packed = jnp.concatenate([stripes[i, :, : count * (i + 1)].transpose(1, 0, 2) for i in range(X)], axis=0)
    return lax.all_gather(packed, COL, axis=0, tiled=True).reshape(-1, TILE)


def to_slot_owner():
    pairs = []
    for place in range(N_ROW):
        for col in range(N_COL):
            owner = col + N_COL * (place // N_COL)
            pairs.append((place * N_COL + col, owner * N_COL + place % N_COL))
    return pairs


def on_device(parent_sigma, slot_tile, slot_count, panel, sep_factor):
    my_row = lax.axis_index(ROW).astype(jnp.int32)
    my_col = lax.axis_index(COL).astype(jnp.int32)
    me = jnp.stack([my_row, my_col])
    sigma = parent_sigma.reshape(4, TILE * 8, TILE)
    with jax.named_scope("front_product"):
        partial = front(slot_tile, slot_count, me, sigma, panel).reshape(N_ROW, WIDTH, 2 * TILE)
    with jax.named_scope("factor_gather"):
        lines, partial = lax.optimization_barrier((spread_lines(sep_factor, my_col), partial))
        shares = gather_factor(lines)
    with jax.named_scope("inverse"):
        inverse = factor_inverse(shares)
    with jax.named_scope("front_sum"):
        pieces = exchange(partial, ROW)
        pieces, inverse = lax.optimization_barrier((pieces, inverse))
        piece = lax.ppermute(total(pieces), ROW + COL, to_slot_owner())
    with jax.named_scope("front_gather"):
        whole = lax.all_gather(piece, COL, axis=0, tiled=True)
    with jax.named_scope("separator"):
        sent = separator(me, slot_count, piece, panel, inverse)
        taken = total(exchange(sent, ROW))
        blocks = exchange(lax.optimization_barrier(spread(taken, N_COL)), COL)
    with jax.named_scope("final"):
        return final(me, slot_count, whole, blocks, inverse)


def solution(mesh):
    inner = Mesh(np.array(mesh.devices).reshape(X, Y, Z, CORE), ROW + COL)
    placed = (
        P(None, ROW, None, None, COL, None),
        P(),
        P(),
        P(ROW, None, None, None),
        P(ROW, None),
    )
    return jax.shard_map(
        on_device,
        mesh=inner,
        in_specs=placed,
        out_specs=(P(ROW, None, None, None), P(ROW, None)),
        check_vma=False,
    )
```

```python
import functools

import jax
import jax.numpy as jnp
import numpy as np
from jax import lax
from jax.experimental import pallas as pl
from jax.experimental.pallas import tpu as pltpu
from jax.sharding import Mesh
from jax.sharding import PartitionSpec as P

ROW = ("x", "y")
COL = ("z", "core")
X, Y, Z, CORE = 4, 8, 8, 2
N_ROW, N_COL = X * Y, Z * CORE
TILE = 128
SEP = 1024
STRIPE = SEP // X
PACKED = STRIPE * X * (X + 1) // 2
WIDTH = SEP // N_COL
OWN = SEP // N_ROW
LINES = OWN // N_COL
MIB = 1024 * 1024
HIGHEST = lax.Precision.HIGHEST


def exact_dot(left, right):
    return jnp.dot(left, right, precision=HIGHEST, preferred_element_type=jnp.float32)


def on_chip(value):
    return pltpu.with_memory_space_constraint(value, pltpu.VMEM)


def off_chip(value):
    return pltpu.with_memory_space_constraint(value, pltpu.HBM)


def front_kernel(tile_ref, count_ref, me_ref, upper_ref, lower_ref, panel_ref, out_ref):
    row, col = me_ref[0], me_ref[1]
    live = [(slot < count_ref[row]).astype(jnp.float32) for slot in range(2)]
    strips = jnp.concatenate([panel_ref[0, slot] * live[slot] for slot in range(2)], axis=0)
    strips_t = strips.T
    for step in range(2):
        owner = col + N_COL * step
        block = jnp.concatenate(
            [
                jnp.concatenate(
                    [sigma[0, pl.ds(tile_ref[owner, slot] * 2 + step, TILE, stride=8), :] for slot in range(2)],
                    axis=1,
                )
                for sigma in (upper_ref, lower_ref)
            ],
            axis=0,
        )
        out_ref[step] = exact_dot(strips_t, block)


def front(slot_tile, slot_count, me, sigma, panel):
    def slab(slot):
        return pl.BlockSpec((1, TILE * 8, TILE), lambda i, tile, count, me: (tile[me[0], slot], 0, 0))

    return pl.pallas_call(
        front_kernel,
        grid_spec=pltpu.PrefetchScalarGridSpec(
            num_scalar_prefetch=3,
            grid=(1,),
            in_specs=[
                slab(0),
                slab(1),
                pl.BlockSpec((1, 2, TILE, SEP), lambda i, *_: (0, 0, 0, 0)),
            ],
            out_specs=pl.BlockSpec((2, SEP, 2 * TILE), lambda i, *_: (0, 0, 0)),
        ),
        out_shape=jax.ShapeDtypeStruct((2, SEP, 2 * TILE), jnp.float32),
        compiler_params=pltpu.CompilerParams(vmem_limit_bytes=16 * MIB),
        name="front",
    )(slot_tile, slot_count, me, off_chip(sigma), off_chip(sigma), off_chip(panel))


def invert_tiles(tiles):
    row = lax.broadcasted_iota(jnp.int32, (TILE, TILE), 0)
    col = lax.broadcasted_iota(jnp.int32, (TILE, TILE), 1)

    def left_of(size):
        return (row // (2 * size) == col // (2 * size)) & (row // size > col // size)

    inverses = []
    for tile in tiles:
        scale = jnp.where(row == col, 1.0 / jnp.where(row == col, tile, 1.0), 0.0)
        down = jnp.sum(scale, axis=1, keepdims=True)
        across = jnp.sum(scale, axis=0, keepdims=True)
        inverses.append(scale - jnp.where(left_of(1), tile * down * across, 0.0))
    size = 2
    while size < TILE:
        mask = left_of(size)
        products = [exact_dot(jnp.where(mask, tile, 0.0), inverse) for tile, inverse in zip(tiles, inverses)]
        inverses = [inverse - exact_dot(inverse, product) for inverse, product in zip(inverses, products)]
        size *= 2
    return inverses


def inverse_kernel(share_ref, out_ref, packed_ref):
    for block in range(PACKED // TILE):
        for y in range(Y):
            for line in range(LINES):
                start = (block * Y + y) * LINES + line
                taken = share_ref[pl.ds(start, N_COL, stride=PACKED // TILE * Y * LINES), :]
                packed_ref[block, pl.ds(y * OWN + line, N_COL, stride=LINES), :] = taken

    def factor(stripe, start, width):
        first = (STRIPE * stripe * (stripe + 1) // 2 + start) // TILE
        return jnp.concatenate([packed_ref[first + block] for block in range(width // TILE)], axis=1)

    diagonals = [factor(stripe, stripe * STRIPE, STRIPE) for stripe in range(X)]
    tiles = [d[p * TILE : (p + 1) * TILE, p * TILE : (p + 1) * TILE] for d in diagonals for p in range(2)]
    inverses = invert_tiles(tiles)
    middles = [exact_dot(d[TILE:, :TILE], inverses[2 * stripe]) for stripe, d in enumerate(diagonals)]
    corners = [-exact_dot(inverses[2 * stripe + 1], middle) for stripe, middle in enumerate(middles)]
    for stripe in range(X):
        top = stripe * STRIPE
        out_ref[top : top + TILE, top : top + TILE] = inverses[2 * stripe]
        out_ref[top : top + TILE, top + TILE :] = jnp.zeros((TILE, SEP - top - TILE), jnp.float32)
        out_ref[top + TILE : top + STRIPE, top : top + TILE] = corners[stripe]
        out_ref[top + TILE : top + STRIPE, top + TILE : top + STRIPE] = inverses[2 * stripe + 1]
        if stripe < X - 1:
            out_ref[top + TILE : top + STRIPE, top + STRIPE :] = jnp.zeros((TILE, SEP - top - STRIPE), jnp.float32)
    products = []
    for stripe in (1, 3):
        left = (stripe - 1) * STRIPE
        above = out_ref[left : left + STRIPE, left : left + STRIPE]
        products.append(exact_dot(factor(stripe, left, STRIPE), above))
    for stripe, product in zip((1, 3), products):
        top = stripe * STRIPE
        own = out_ref[top : top + STRIPE, top : top + STRIPE]
        out_ref[top : top + STRIPE, top - STRIPE : top] = -exact_dot(own, product)
    half = 2 * STRIPE
    left_part = jnp.concatenate([factor(2, 0, half), factor(3, 0, half)], axis=0)
    first_cols = exact_dot(left_part, out_ref[:half, :STRIPE])
    last_cols = exact_dot(left_part[:, STRIPE:], out_ref[STRIPE:half, STRIPE:half])
    product = jnp.concatenate([first_cols, last_cols], axis=1)
    out_ref[half : half + STRIPE, :half] = -exact_dot(out_ref[half : half + STRIPE, half : half + STRIPE], product[:STRIPE])
    out_ref[half + STRIPE :, :half] = -exact_dot(out_ref[half + STRIPE :, half:], product)


VMEM = pl.BlockSpec(memory_space=pltpu.VMEM)
SMEM = pl.BlockSpec(memory_space=pltpu.SMEM)


def factor_inverse(shares):
    return pl.pallas_call(
        inverse_kernel,
        in_specs=[VMEM],
        out_specs=VMEM,
        out_shape=jax.ShapeDtypeStruct((SEP, SEP), jnp.float32),
        scratch_shapes=[pltpu.VMEM((PACKED // TILE, STRIPE, TILE), jnp.float32)],
        compiler_params=pltpu.CompilerParams(vmem_limit_bytes=20 * MIB),
        name="factor_inverse",
    )(shares)


def times_inverse(left_ref, inverse_ref, stripe):
    start = stripe * STRIPE
    return exact_dot(left_ref[:, start:], inverse_ref[start:, :])


def for_stripe(body):
    for stripe in range(X):
        pl.when(pl.program_id(0) == stripe)(functools.partial(body, stripe))


def whole_block(shape):
    return pl.BlockSpec(shape, lambda i: (0,) * len(shape))


def separator_kernel(me_ref, count_ref, piece_ref, panel_ref, inverse_ref, out_ref):
    row, col = me_ref[0], me_ref[1]
    live = [(slot < count_ref[row]).astype(jnp.float32) for slot in range(2)]
    strips = jnp.concatenate([panel_ref[0, slot] * live[slot] for slot in range(2)], axis=0)
    local = exact_dot(piece_ref[...], strips)
    down = lax.broadcasted_iota(jnp.int32, (WIDTH, SEP), 0) + col * WIDTH
    across = lax.broadcasted_iota(jnp.int32, (WIDTH, SEP), 1)
    local = local + jnp.where((down == across) & (row == 0), 1.0, 0.0)
    for stripe in range(X):
        first = stripe * STRIPE
        turned = exact_dot(local[:, first:], inverse_ref[first:, first : first + STRIPE]).T
        for place in range(STRIPE // OWN):
            start = place * OWN
            out_ref[stripe * (STRIPE // OWN) + place] = jnp.concatenate(
                [turned[start : start + OWN // 2], turned[start + OWN // 2 : start + OWN]], axis=1
            )


def separator(me, slot_count, piece, panel, inverse):
    return pl.pallas_call(
        separator_kernel,
        in_specs=[SMEM, SMEM, VMEM, VMEM, VMEM],
        out_specs=VMEM,
        out_shape=jax.ShapeDtypeStruct((N_ROW, OWN // 2, 2 * WIDTH), jnp.float32),
        compiler_params=pltpu.CompilerParams(vmem_limit_bytes=14 * MIB),
        name="separator",
    )(me, slot_count, piece, panel, inverse)


def final_kernel(me_ref, count_ref, whole_ref, blocks_ref, inverse_ref, update_ref, sep_ref, left_ref):
    @pl.when(pl.program_id(0) == 0)
    def _():
        row = me_ref[0]
        turned = whole_ref[...].T
        for slot in range(2):
            sign = -(slot < count_ref[row]).astype(jnp.float32)
            left_ref[slot * TILE : (slot + 1) * TILE, :] = turned[slot * TILE : (slot + 1) * TILE] * sign
        for side in range(2):
            lanes = slice(side * WIDTH, (side + 1) * WIDTH)
            start = 2 * TILE + side * (OWN // 2)
            left_ref[start : start + OWN // 2, :] = jnp.concatenate(
                [blocks_ref[place][:, lanes] for place in range(N_COL)], axis=1
            )

    @for_stripe
    def _(stripe):
        result = times_inverse(left_ref, inverse_ref, stripe)
        update_ref[0, 0] = result[:TILE]
        update_ref[0, 1] = result[TILE : 2 * TILE]
        sep_ref[...] = result[2 * TILE :]


def final(me, slot_count, whole, blocks, inverse):
    return pl.pallas_call(
        final_kernel,
        grid=(X,),
        in_specs=[
            SMEM,
            SMEM,
            whole_block((SEP, 2 * TILE)),
            whole_block((N_COL, OWN // 2, 2 * WIDTH)),
            pl.BlockSpec((SEP, STRIPE), lambda i: (0, i)),
        ],
        out_specs=(
            pl.BlockSpec((1, 2, TILE, STRIPE), lambda i: (0, 0, 0, i)),
            pl.BlockSpec((OWN, STRIPE), lambda i: (0, i)),
        ),
        out_shape=(
            jax.ShapeDtypeStruct((1, 2, TILE, SEP), jnp.float32),
            jax.ShapeDtypeStruct((OWN, SEP), jnp.float32),
        ),
        scratch_shapes=[pltpu.VMEM((2 * TILE + OWN, SEP), jnp.float32)],
        compiler_params=pltpu.CompilerParams(vmem_limit_bytes=16 * MIB),
        name="final",
    )(me, slot_count, off_chip(whole), blocks, off_chip(inverse))


def total_kernel(pieces_ref, out_ref):
    out_ref[...] = jnp.sum(pieces_ref[...], axis=0)


def total(pieces):
    return pl.pallas_call(
        total_kernel,
        in_specs=[VMEM],
        out_specs=VMEM,
        out_shape=jax.ShapeDtypeStruct(pieces.shape[1:], jnp.float32),
        compiler_params=pltpu.CompilerParams(vmem_limit_bytes=8 * MIB),
        name="total",
    )(on_chip(pieces))


def spread(value, size):
    return jnp.broadcast_to(value[None], (size, *value.shape))


def exchange(blocks, axis):
    return lax.all_to_all(blocks, axis, 0, 0, tiled=True)


def spread_lines(sep_factor, col):
    return exchange(spread(lax.dynamic_slice_in_dim(sep_factor, col * LINES, LINES, 0), N_ROW), ROW)


def gather_factor(lines):
    stripes = lines.reshape(X, Y * LINES, SEP // TILE, TILE)
    count = STRIPE // TILE
    packed = jnp.concatenate([stripes[i, :, : count * (i + 1)].transpose(1, 0, 2) for i in range(X)], axis=0)
    return lax.all_gather(packed, COL, axis=0, tiled=True).reshape(-1, TILE)


def to_slot_owner():
    pairs = []
    for place in range(N_ROW):
        for col in range(N_COL):
            owner = col + N_COL * (place // N_COL)
            pairs.append((place * N_COL + col, owner * N_COL + place % N_COL))
    return pairs


def on_device(parent_sigma, slot_tile, slot_count, panel, sep_factor):
    my_row = lax.axis_index(ROW).astype(jnp.int32)
    my_col = lax.axis_index(COL).astype(jnp.int32)
    me = jnp.stack([my_row, my_col])
    sigma = parent_sigma.reshape(4, TILE * 8, TILE)
    with jax.named_scope("front_product"):
        partial = front(slot_tile, slot_count, me, sigma, panel).reshape(N_ROW, WIDTH, 2 * TILE)
    with jax.named_scope("factor_gather"):
        lines, partial = lax.optimization_barrier((spread_lines(sep_factor, my_col), partial))
        shares = gather_factor(lines)
    with jax.named_scope("front_sum"):
        half = total(exchange(partial.reshape(X, Y, WIDTH, 2 * TILE), "x"))
        piece = total(exchange(half, "y"))
        piece = lax.ppermute(piece, ROW + COL, to_slot_owner())
    with jax.named_scope("front_gather"):
        whole = lax.all_gather(piece, COL, axis=0, tiled=True)
    with jax.named_scope("inverse"):
        shares, _ = lax.optimization_barrier((shares, piece))
        inverse = factor_inverse(shares)
    with jax.named_scope("separator"):
        sent = separator(me, slot_count, piece, panel, inverse)
        taken = total(exchange(sent, ROW))
        blocks = exchange(lax.optimization_barrier(spread(taken, N_COL)), COL)
    with jax.named_scope("final"):
        return final(me, slot_count, whole, blocks, inverse)


def solution(mesh):
    inner = Mesh(np.array(mesh.devices).reshape(X, Y, Z, CORE), ROW + COL)
    placed = (
        P(None, ROW, None, None, COL, None),
        P(),
        P(),
        P(ROW, None, None, None),
        P(ROW, None),
    )
    return jax.shard_map(
        on_device,
        mesh=inner,
        in_specs=placed,
        out_specs=(P(ROW, None, None, None), P(ROW, None)),
        check_vma=False,
    )
```

```python
import functools

import jax
import jax.numpy as jnp
import numpy as np
from jax import lax
from jax.experimental import pallas as pl
from jax.experimental.pallas import tpu as pltpu
from jax.sharding import Mesh
from jax.sharding import PartitionSpec as P

ROW = ("x", "y")
COL = ("far", "near", "core")
X, Y, FAR, NEAR, CORE = 4, 8, 4, 2, 2
Z = FAR * NEAR
N_ROW, N_COL = X * Y, Z * CORE
SHARES = NEAR * CORE
SWAP = [(0, 1), (1, 0)]
TILE = 128
SEP = 1024
STRIPE = SEP // X
PACKED = STRIPE * X * (X + 1) // 2
WIDTH = SEP // N_COL
OWN = SEP // N_ROW
LINES = OWN // SHARES
MIB = 1024 * 1024
HIGHEST = lax.Precision.HIGHEST


def exact_dot(left, right):
    return jnp.dot(left, right, precision=HIGHEST, preferred_element_type=jnp.float32)


def on_chip(value):
    return pltpu.with_memory_space_constraint(value, pltpu.VMEM)


def off_chip(value):
    return pltpu.with_memory_space_constraint(value, pltpu.HBM)


def front_kernel(tile_ref, count_ref, me_ref, upper_ref, lower_ref, panel_ref, out_ref):
    row, col = me_ref[0], me_ref[1]
    live = [(slot < count_ref[row]).astype(jnp.float32) for slot in range(2)]
    strips = jnp.concatenate([panel_ref[0, slot] * live[slot] for slot in range(2)], axis=0)
    strips_t = strips.T
    for step in range(2):
        owner = col + N_COL * step
        block = jnp.concatenate(
            [
                jnp.concatenate(
                    [sigma[0, pl.ds(tile_ref[owner, slot] * 2 + step, TILE, stride=8), :] for slot in range(2)],
                    axis=1,
                )
                for sigma in (upper_ref, lower_ref)
            ],
            axis=0,
        )
        out_ref[step] = exact_dot(strips_t, block)


def front(slot_tile, slot_count, me, sigma, panel):
    def slab(slot):
        return pl.BlockSpec((1, TILE * 8, TILE), lambda i, tile, count, me: (tile[me[0], slot], 0, 0))

    return pl.pallas_call(
        front_kernel,
        grid_spec=pltpu.PrefetchScalarGridSpec(
            num_scalar_prefetch=3,
            grid=(1,),
            in_specs=[
                slab(0),
                slab(1),
                pl.BlockSpec((1, 2, TILE, SEP), lambda i, *_: (0, 0, 0, 0)),
            ],
            out_specs=pl.BlockSpec((2, SEP, 2 * TILE), lambda i, *_: (0, 0, 0)),
        ),
        out_shape=jax.ShapeDtypeStruct((2, SEP, 2 * TILE), jnp.float32),
        compiler_params=pltpu.CompilerParams(vmem_limit_bytes=16 * MIB),
        name="front",
    )(slot_tile, slot_count, me, off_chip(sigma), off_chip(sigma), off_chip(panel))


def invert_tiles(tiles):
    row = lax.broadcasted_iota(jnp.int32, (TILE, TILE), 0)
    col = lax.broadcasted_iota(jnp.int32, (TILE, TILE), 1)

    def left_of(size):
        return (row // (2 * size) == col // (2 * size)) & (row // size > col // size)

    inverses = []
    for tile in tiles:
        scale = jnp.where(row == col, 1.0 / jnp.where(row == col, tile, 1.0), 0.0)
        down = jnp.sum(scale, axis=1, keepdims=True)
        across = jnp.sum(scale, axis=0, keepdims=True)
        inverses.append(scale - jnp.where(left_of(1), tile * down * across, 0.0))
    size = 2
    while size < TILE:
        mask = left_of(size)
        products = [exact_dot(jnp.where(mask, tile, 0.0), inverse) for tile, inverse in zip(tiles, inverses)]
        inverses = [inverse - exact_dot(inverse, product) for inverse, product in zip(inverses, products)]
        size *= 2
    return inverses


def inverse_kernel(me_ref, *refs):
    share_refs, out_ref, packed_ref = refs[:SHARES], refs[SHARES], refs[SHARES + 1]
    near, core = me_ref[2], me_ref[3]
    for index, share_ref in enumerate(share_refs):
        owner = lax.rem(near + index // CORE, NEAR) * CORE + lax.rem(core + index % CORE, CORE)
        for y in range(Y):
            start = pl.multiple_of(y * OWN + owner * LINES, LINES)
            packed_ref[pl.ds(start, LINES), :] = share_ref[y * LINES : (y + 1) * LINES, :]

    def factor(stripe, start, width):
        base = STRIPE * stripe * (stripe + 1) // 2
        return packed_ref[:, base + start : base + start + width]

    diagonals = [factor(stripe, stripe * STRIPE, STRIPE) for stripe in range(X)]
    tiles = [d[p * TILE : (p + 1) * TILE, p * TILE : (p + 1) * TILE] for d in diagonals for p in range(2)]
    inverses = invert_tiles(tiles)
    middles = [exact_dot(d[TILE:, :TILE], inverses[2 * stripe]) for stripe, d in enumerate(diagonals)]
    corners = [-exact_dot(inverses[2 * stripe + 1], middle) for stripe, middle in enumerate(middles)]
    for stripe in range(X):
        top = stripe * STRIPE
        out_ref[top : top + TILE, top : top + TILE] = inverses[2 * stripe]
        out_ref[top : top + TILE, top + TILE :] = jnp.zeros((TILE, SEP - top - TILE), jnp.float32)
        out_ref[top + TILE : top + STRIPE, top : top + TILE] = corners[stripe]
        out_ref[top + TILE : top + STRIPE, top + TILE : top + STRIPE] = inverses[2 * stripe + 1]
        if stripe < X - 1:
            out_ref[top + TILE : top + STRIPE, top + STRIPE :] = jnp.zeros((TILE, SEP - top - STRIPE), jnp.float32)
    products = []
    for stripe in (1, 3):
        left = (stripe - 1) * STRIPE
        above = out_ref[left : left + STRIPE, left : left + STRIPE]
        products.append(exact_dot(factor(stripe, left, STRIPE), above))
    for stripe, product in zip((1, 3), products):
        top = stripe * STRIPE
        own = out_ref[top : top + STRIPE, top : top + STRIPE]
        out_ref[top : top + STRIPE, top - STRIPE : top] = -exact_dot(own, product)
    half = 2 * STRIPE
    left_part = jnp.concatenate([factor(2, 0, half), factor(3, 0, half)], axis=0)
    first_cols = exact_dot(left_part, out_ref[:half, :STRIPE])
    last_cols = exact_dot(left_part[:, STRIPE:], out_ref[STRIPE:half, STRIPE:half])
    product = jnp.concatenate([first_cols, last_cols], axis=1)
    out_ref[half : half + STRIPE, :half] = -exact_dot(out_ref[half : half + STRIPE, half : half + STRIPE], product[:STRIPE])
    out_ref[half + STRIPE :, :half] = -exact_dot(out_ref[half + STRIPE :, half:], product)


VMEM = pl.BlockSpec(memory_space=pltpu.VMEM)
SMEM = pl.BlockSpec(memory_space=pltpu.SMEM)


def factor_inverse(me, shares):
    return pl.pallas_call(
        inverse_kernel,
        in_specs=[SMEM] + [VMEM] * SHARES,
        out_specs=VMEM,
        out_shape=jax.ShapeDtypeStruct((SEP, SEP), jnp.float32),
        scratch_shapes=[pltpu.VMEM((STRIPE, PACKED), jnp.float32)],
        compiler_params=pltpu.CompilerParams(vmem_limit_bytes=20 * MIB),
        name="factor_inverse",
    )(me, *shares)


def times_inverse(left_ref, inverse_ref, stripe):
    start = stripe * STRIPE
    return exact_dot(left_ref[:, start:], inverse_ref[start:, :])


def for_stripe(body):
    for stripe in range(X):
        pl.when(pl.program_id(0) == stripe)(functools.partial(body, stripe))


def whole_block(shape):
    return pl.BlockSpec(shape, lambda i: (0,) * len(shape))


def separator_kernel(me_ref, count_ref, piece_ref, panel_ref, inverse_ref, out_ref):
    row, col = me_ref[0], me_ref[1]
    live = [(slot < count_ref[row]).astype(jnp.float32) for slot in range(2)]
    strips = jnp.concatenate([panel_ref[0, slot] * live[slot] for slot in range(2)], axis=0)
    piece = jnp.concatenate([piece_ref[:WIDTH], piece_ref[WIDTH:]], axis=1)
    local = exact_dot(piece, strips)
    down = lax.broadcasted_iota(jnp.int32, (WIDTH, SEP), 0) + col * WIDTH
    across = lax.broadcasted_iota(jnp.int32, (WIDTH, SEP), 1)
    local = local + jnp.where((down == across) & (row == 0), 1.0, 0.0)
    for stripe in range(X):
        first = stripe * STRIPE
        turned = exact_dot(local[:, first:], inverse_ref[first:, first : first + STRIPE]).T
        for place in range(STRIPE // OWN):
            start = place * OWN
            out_ref[stripe * (STRIPE // OWN) + place] = jnp.concatenate(
                [turned[start : start + OWN // 2], turned[start + OWN // 2 : start + OWN]], axis=1
            )


def separator(me, slot_count, piece, panel, inverse):
    return pl.pallas_call(
        separator_kernel,
        in_specs=[SMEM, SMEM, VMEM, VMEM, VMEM],
        out_specs=VMEM,
        out_shape=jax.ShapeDtypeStruct((N_ROW, OWN // 2, 2 * WIDTH), jnp.float32),
        compiler_params=pltpu.CompilerParams(vmem_limit_bytes=14 * MIB),
        name="separator",
    )(me, slot_count, piece, panel, inverse)


def final_kernel(me_ref, count_ref, low_ref, high_ref, inverse_ref, update_ref, sep_ref, left_ref):
    @pl.when(pl.program_id(0) == 0)
    def _():
        row = me_ref[0]
        blocks = [ref[core, z] for ref in (low_ref, high_ref) for z in range(Z // 2) for core in range(CORE)]
        for slot in range(2):
            sign = -(slot < count_ref[row]).astype(jnp.float32)
            whole = jnp.concatenate([block[slot * WIDTH : (slot + 1) * WIDTH] for block in blocks], axis=0)
            left_ref[slot * TILE : (slot + 1) * TILE, :] = whole.T * sign
        for side in range(2):
            lanes = slice(side * WIDTH, (side + 1) * WIDTH)
            start = 2 * TILE + side * (OWN // 2)
            left_ref[start : start + OWN // 2, :] = jnp.concatenate(
                [block[2 * WIDTH :, lanes] for block in blocks], axis=1
            )

    @for_stripe
    def _(stripe):
        result = times_inverse(left_ref, inverse_ref, stripe)
        update_ref[0, 0] = result[:TILE]
        update_ref[0, 1] = result[TILE : 2 * TILE]
        sep_ref[...] = result[2 * TILE :]


def final(me, slot_count, low, high, inverse):
    return pl.pallas_call(
        final_kernel,
        grid=(X,),
        in_specs=[
            SMEM,
            SMEM,
            whole_block(low.shape),
            whole_block(high.shape),
            pl.BlockSpec((SEP, STRIPE), lambda i: (0, i)),
        ],
        out_specs=(
            pl.BlockSpec((1, 2, TILE, STRIPE), lambda i: (0, 0, 0, i)),
            pl.BlockSpec((OWN, STRIPE), lambda i: (0, i)),
        ),
        out_shape=(
            jax.ShapeDtypeStruct((1, 2, TILE, SEP), jnp.float32),
            jax.ShapeDtypeStruct((OWN, SEP), jnp.float32),
        ),
        scratch_shapes=[pltpu.VMEM((2 * TILE + OWN, SEP), jnp.float32)],
        compiler_params=pltpu.CompilerParams(vmem_limit_bytes=16 * MIB),
        name="final",
    )(me, slot_count, low, high, off_chip(inverse))


def total_kernel(pieces_ref, out_ref):
    summed = jnp.sum(pieces_ref[...], axis=0)
    rows = summed.shape[-2]
    if summed.shape[-1] == out_ref.shape[-1]:
        out_ref[...] = summed
    else:
        out_ref[:rows] = summed[:, :TILE]
        out_ref[rows:] = summed[:, TILE:]


def total(pieces, split=False):
    shape = (2 * pieces.shape[1], TILE) if split else pieces.shape[1:]
    return pl.pallas_call(
        total_kernel,
        in_specs=[VMEM],
        out_specs=VMEM,
        out_shape=jax.ShapeDtypeStruct(shape, jnp.float32),
        compiler_params=pltpu.CompilerParams(vmem_limit_bytes=8 * MIB),
        name="total",
    )(on_chip(pieces))


def spread(value, size):
    return jnp.broadcast_to(value[None], (size, *value.shape))


def exchange(blocks, axis):
    return lax.all_to_all(blocks, axis, 0, 0, tiled=True)


def spread_lines(sep_factor, share):
    return exchange(spread(lax.dynamic_slice_in_dim(sep_factor, share * LINES, LINES, 0), N_ROW), ROW)


def gather_factor(lines):
    stripes = lines.reshape(X, Y * LINES, SEP)
    packed = jnp.concatenate([stripes[i][:, : STRIPE * (i + 1)] for i in range(X)], axis=1)
    return packed, lax.ppermute(packed, "core", SWAP), lax.ppermute(packed, "near", SWAP)


def gather_blocks(block):
    blocks = exchange(spread(block, Z), ("far", "near"))
    return tuple(lax.all_gather(half, "core", axis=0) for half in (blocks[: Z // 2], blocks[Z // 2 :]))


def to_slot_owner():
    pairs = []
    for place in range(N_ROW):
        for col in range(N_COL):
            owner = col + N_COL * (place // N_COL)
            pairs.append((place * N_COL + col, owner * N_COL + place % N_COL))
    return pairs


def on_device(parent_sigma, slot_tile, slot_count, panel, sep_factor):
    my_row = lax.axis_index(ROW).astype(jnp.int32)
    my_col = lax.axis_index(COL).astype(jnp.int32)
    near = lax.axis_index("near").astype(jnp.int32)
    core = lax.axis_index("core").astype(jnp.int32)
    me = jnp.stack([my_row, my_col, near, core])
    sigma = parent_sigma.reshape(4, TILE * 8, TILE)
    with jax.named_scope("front_product"):
        partial = front(slot_tile, slot_count, me, sigma, panel).reshape(X, Y, WIDTH, 2 * TILE)
    with jax.named_scope("factor_gather"):
        lines, partial = lax.optimization_barrier((spread_lines(sep_factor, near * CORE + core), partial))
        shares = gather_factor(lines)
    with jax.named_scope("front_sum"):
        pieces, near_share = lax.optimization_barrier((exchange(partial, "x"), shares[2]))
        half = total(pieces)
        shares = (*shares[:2], near_share, lax.ppermute(near_share, "core", SWAP))
        pieces = exchange(half, "y")
    with jax.named_scope("inverse"):
        shares, _ = lax.optimization_barrier((shares, half))
        inverse = factor_inverse(me, shares)
    with jax.named_scope("front_place"):
        pieces, inverse = lax.optimization_barrier((pieces, inverse))
        piece = lax.ppermute(total(pieces, split=True), ROW + COL, to_slot_owner())
    with jax.named_scope("separator"):
        sent = separator(me, slot_count, piece, panel, inverse)
        taken = total(exchange(sent, ROW))
    with jax.named_scope("gather"):
        low, high = gather_blocks(jnp.concatenate([piece, taken], axis=0))
    with jax.named_scope("final"):
        return final(me, slot_count, low, high, inverse)


def solution(mesh):
    inner = Mesh(np.array(mesh.devices).reshape(X, Y, FAR, NEAR, CORE), ROW + COL)
    placed = (
        P(None, ROW, None, None, COL, None),
        P(),
        P(),
        P(ROW, None, None, None),
        P(ROW, None),
    )
    return jax.shard_map(
        on_device,
        mesh=inner,
        in_specs=placed,
        out_specs=(P(ROW, None, None, None), P(ROW, None)),
        check_vma=False,
    )
```

```python
import functools

import jax
import jax.numpy as jnp
import numpy as np
from jax import lax
from jax.experimental import pallas as pl
from jax.experimental.pallas import tpu as pltpu
from jax.sharding import Mesh
from jax.sharding import PartitionSpec as P

ROW = ("x", "y")
COL = ("z", "core")
X, Y, Z, CORE = 4, 8, 8, 2
N_ROW, N_COL = X * Y, Z * CORE
TILE = 128
SEP = 1024
STRIPE = SEP // X
PACKED = STRIPE * X * (X + 1) // 2
WIDTH = SEP // N_COL
OWN = SEP // N_ROW
LINES = OWN // N_COL
MIB = 1024 * 1024


def split(value):
    high = value.astype(jnp.bfloat16)
    return high, (value - high.astype(jnp.float32)).astype(jnp.bfloat16)


def split_dot(left, right):
    def dot(first, last):
        return jnp.dot(first, last, preferred_element_type=jnp.float32)

    (left_high, left_low), (right_high, right_low) = left, right
    return dot(left_high, right_high) + (dot(left_high, right_low) + dot(left_low, right_high))


def fine_dot(left, right):
    return split_dot(split(left), split(right))


def on_chip(value):
    return pltpu.with_memory_space_constraint(value, pltpu.VMEM)


def off_chip(value):
    return pltpu.with_memory_space_constraint(value, pltpu.HBM)


def front_kernel(tile_ref, count_ref, me_ref, upper_ref, lower_ref, panel_ref, out_ref):
    row, col = me_ref[0], me_ref[1]
    live = [(slot < count_ref[row]).astype(jnp.float32) for slot in range(2)]
    strips = jnp.concatenate([panel_ref[0, slot] * live[slot] for slot in range(2)], axis=0)
    strips_t = strips.T
    for step in range(2):
        owner = col + N_COL * step
        block = jnp.concatenate(
            [
                jnp.concatenate(
                    [sigma[0, pl.ds(tile_ref[owner, slot] * 2 + step, TILE, stride=8), :] for slot in range(2)],
                    axis=1,
                )
                for sigma in (upper_ref, lower_ref)
            ],
            axis=0,
        )
        out_ref[step] = fine_dot(strips_t, block)


def front(slot_tile, slot_count, me, sigma, panel):
    def slab(slot):
        return pl.BlockSpec((1, TILE * 8, TILE), lambda i, tile, count, me: (tile[me[0], slot], 0, 0))

    return pl.pallas_call(
        front_kernel,
        grid_spec=pltpu.PrefetchScalarGridSpec(
            num_scalar_prefetch=3,
            grid=(1,),
            in_specs=[
                slab(0),
                slab(1),
                pl.BlockSpec((1, 2, TILE, SEP), lambda i, *_: (0, 0, 0, 0)),
            ],
            out_specs=pl.BlockSpec((2, SEP, 2 * TILE), lambda i, *_: (0, 0, 0)),
        ),
        out_shape=jax.ShapeDtypeStruct((2, SEP, 2 * TILE), jnp.float32),
        compiler_params=pltpu.CompilerParams(vmem_limit_bytes=16 * MIB),
        name="front",
    )(slot_tile, slot_count, me, off_chip(sigma), off_chip(sigma), off_chip(panel))


def invert_tiles(tiles):
    row = lax.broadcasted_iota(jnp.int32, (TILE, TILE), 0)
    col = lax.broadcasted_iota(jnp.int32, (TILE, TILE), 1)

    def left_of(size):
        return (row // (2 * size) == col // (2 * size)) & (row // size > col // size)

    inverses = []
    for tile in tiles:
        scale = jnp.where(row == col, 1.0 / jnp.where(row == col, tile, 1.0), 0.0)
        down = jnp.sum(scale, axis=1, keepdims=True)
        across = jnp.sum(scale, axis=0, keepdims=True)
        inverses.append(scale - jnp.where(left_of(1), tile * down * across, 0.0))
    size = 2
    while size < TILE:
        mask = left_of(size)
        halves = [split(inverse) for inverse in inverses]
        products = [split_dot(split(jnp.where(mask, tile, 0.0)), half) for tile, half in zip(tiles, halves)]
        inverses = [
            inverse - split_dot(half, split(product)) for inverse, half, product in zip(inverses, halves, products)
        ]
        size *= 2
    return inverses


def inverse_kernel(share_ref, out_ref, packed_ref):
    for block in range(PACKED // TILE):
        for y in range(Y):
            for line in range(LINES):
                start = (block * Y + y) * LINES + line
                taken = share_ref[pl.ds(start, N_COL, stride=PACKED // TILE * Y * LINES), :]
                packed_ref[block, pl.ds(y * OWN + line, N_COL, stride=LINES), :] = taken

    def factor(stripe, start, width):
        first = (STRIPE * stripe * (stripe + 1) // 2 + start) // TILE
        return jnp.concatenate([packed_ref[first + block] for block in range(width // TILE)], axis=1)

    diagonals = [factor(stripe, stripe * STRIPE, STRIPE) for stripe in range(X)]
    tiles = [d[p * TILE : (p + 1) * TILE, p * TILE : (p + 1) * TILE] for d in diagonals for p in range(2)]
    inverses = invert_tiles(tiles)
    middles = [fine_dot(d[TILE:, :TILE], inverses[2 * stripe]) for stripe, d in enumerate(diagonals)]
    corners = [-fine_dot(inverses[2 * stripe + 1], middle) for stripe, middle in enumerate(middles)]
    for stripe in range(X):
        top = stripe * STRIPE
        out_ref[top : top + TILE, top : top + TILE] = inverses[2 * stripe]
        out_ref[top : top + TILE, top + TILE :] = jnp.zeros((TILE, SEP - top - TILE), jnp.float32)
        out_ref[top + TILE : top + STRIPE, top : top + TILE] = corners[stripe]
        out_ref[top + TILE : top + STRIPE, top + TILE : top + STRIPE] = inverses[2 * stripe + 1]
        if stripe < X - 1:
            out_ref[top + TILE : top + STRIPE, top + STRIPE :] = jnp.zeros((TILE, SEP - top - STRIPE), jnp.float32)
    products = []
    for stripe in (1, 3):
        left = (stripe - 1) * STRIPE
        above = out_ref[left : left + STRIPE, left : left + STRIPE]
        products.append(fine_dot(factor(stripe, left, STRIPE), above))
    for stripe, product in zip((1, 3), products):
        top = stripe * STRIPE
        own = out_ref[top : top + STRIPE, top : top + STRIPE]
        out_ref[top : top + STRIPE, top - STRIPE : top] = -fine_dot(own, product)
    half = 2 * STRIPE
    left_part = jnp.concatenate([factor(2, 0, half), factor(3, 0, half)], axis=0)
    first_cols = fine_dot(left_part, out_ref[:half, :STRIPE])
    last_cols = fine_dot(left_part[:, STRIPE:], out_ref[STRIPE:half, STRIPE:half])
    product = jnp.concatenate([first_cols, last_cols], axis=1)
    out_ref[half : half + STRIPE, :half] = -fine_dot(out_ref[half : half + STRIPE, half : half + STRIPE], product[:STRIPE])
    out_ref[half + STRIPE :, :half] = -fine_dot(out_ref[half + STRIPE :, half:], product)


VMEM = pl.BlockSpec(memory_space=pltpu.VMEM)
SMEM = pl.BlockSpec(memory_space=pltpu.SMEM)


def factor_inverse(shares):
    return pl.pallas_call(
        inverse_kernel,
        in_specs=[VMEM],
        out_specs=VMEM,
        out_shape=jax.ShapeDtypeStruct((SEP, SEP), jnp.float32),
        scratch_shapes=[pltpu.VMEM((PACKED // TILE, STRIPE, TILE), jnp.float32)],
        compiler_params=pltpu.CompilerParams(vmem_limit_bytes=20 * MIB),
        name="factor_inverse",
    )(shares)


def times_inverse(left_ref, inverse_ref, stripe):
    start = stripe * STRIPE
    return fine_dot(left_ref[:, start:], inverse_ref[start:, :])


def for_stripe(body):
    for stripe in range(X):
        pl.when(pl.program_id(0) == stripe)(functools.partial(body, stripe))


def whole_block(shape):
    return pl.BlockSpec(shape, lambda i: (0,) * len(shape))


def separator_kernel(me_ref, count_ref, piece_ref, panel_ref, inverse_ref, out_ref):
    row, col = me_ref[0], me_ref[1]
    live = [(slot < count_ref[row]).astype(jnp.float32) for slot in range(2)]
    strips = jnp.concatenate([panel_ref[0, slot] * live[slot] for slot in range(2)], axis=0)
    local = fine_dot(piece_ref[...], strips)
    down = lax.broadcasted_iota(jnp.int32, (WIDTH, SEP), 0) + col * WIDTH
    across = lax.broadcasted_iota(jnp.int32, (WIDTH, SEP), 1)
    local = local + jnp.where((down == across) & (row == 0), 1.0, 0.0)
    for stripe in range(X):
        first = stripe * STRIPE
        turned = fine_dot(local[:, first:], inverse_ref[first:, first : first + STRIPE]).T
        for place in range(STRIPE // OWN):
            start = place * OWN
            out_ref[stripe * (STRIPE // OWN) + place] = jnp.concatenate(
                [turned[start : start + OWN // 2], turned[start + OWN // 2 : start + OWN]], axis=1
            )


def separator(me, slot_count, piece, panel, inverse):
    return pl.pallas_call(
        separator_kernel,
        in_specs=[SMEM, SMEM, VMEM, VMEM, VMEM],
        out_specs=VMEM,
        out_shape=jax.ShapeDtypeStruct((N_ROW, OWN // 2, 2 * WIDTH), jnp.float32),
        compiler_params=pltpu.CompilerParams(vmem_limit_bytes=14 * MIB),
        name="separator",
    )(me, slot_count, piece, panel, inverse)


def final_kernel(me_ref, count_ref, whole_ref, blocks_ref, inverse_ref, update_ref, sep_ref, left_ref):
    @pl.when(pl.program_id(0) == 0)
    def _():
        row = me_ref[0]
        turned = whole_ref[...].T
        for slot in range(2):
            sign = -(slot < count_ref[row]).astype(jnp.float32)
            left_ref[slot * TILE : (slot + 1) * TILE, :] = turned[slot * TILE : (slot + 1) * TILE] * sign
        for side in range(2):
            lanes = slice(side * WIDTH, (side + 1) * WIDTH)
            start = 2 * TILE + side * (OWN // 2)
            left_ref[start : start + OWN // 2, :] = jnp.concatenate(
                [blocks_ref[place][:, lanes] for place in range(N_COL)], axis=1
            )

    @for_stripe
    def _(stripe):
        result = times_inverse(left_ref, inverse_ref, stripe)
        update_ref[0, 0] = result[:TILE]
        update_ref[0, 1] = result[TILE : 2 * TILE]
        sep_ref[...] = result[2 * TILE :]


def final(me, slot_count, whole, blocks, inverse):
    return pl.pallas_call(
        final_kernel,
        grid=(X,),
        in_specs=[
            SMEM,
            SMEM,
            whole_block((SEP, 2 * TILE)),
            whole_block((N_COL, OWN // 2, 2 * WIDTH)),
            pl.BlockSpec((SEP, STRIPE), lambda i: (0, i)),
        ],
        out_specs=(
            pl.BlockSpec((1, 2, TILE, STRIPE), lambda i: (0, 0, 0, i)),
            pl.BlockSpec((OWN, STRIPE), lambda i: (0, i)),
        ),
        out_shape=(
            jax.ShapeDtypeStruct((1, 2, TILE, SEP), jnp.float32),
            jax.ShapeDtypeStruct((OWN, SEP), jnp.float32),
        ),
        scratch_shapes=[pltpu.VMEM((2 * TILE + OWN, SEP), jnp.float32)],
        compiler_params=pltpu.CompilerParams(vmem_limit_bytes=16 * MIB),
        name="final",
    )(me, slot_count, off_chip(whole), blocks, off_chip(inverse))


def total_kernel(pieces_ref, out_ref):
    out_ref[...] = jnp.sum(pieces_ref[...], axis=0)


def total(pieces):
    return pl.pallas_call(
        total_kernel,
        in_specs=[VMEM],
        out_specs=VMEM,
        out_shape=jax.ShapeDtypeStruct(pieces.shape[1:], jnp.float32),
        compiler_params=pltpu.CompilerParams(vmem_limit_bytes=8 * MIB),
        name="total",
    )(on_chip(pieces))


def spread(value, size):
    return jnp.broadcast_to(value[None], (size, *value.shape))


def exchange(blocks, axis):
    return lax.all_to_all(blocks, axis, 0, 0, tiled=True)


def spread_lines(sep_factor, col):
    return exchange(spread(lax.dynamic_slice_in_dim(sep_factor, col * LINES, LINES, 0), N_ROW), ROW)


def gather_factor(lines):
    stripes = lines.reshape(X, Y * LINES, SEP // TILE, TILE)
    count = STRIPE // TILE
    packed = jnp.concatenate([stripes[i, :, : count * (i + 1)].transpose(1, 0, 2) for i in range(X)], axis=0)
    return lax.all_gather(packed, COL, axis=0, tiled=True).reshape(-1, TILE)


def to_slot_owner():
    pairs = []
    for place in range(N_ROW):
        for col in range(N_COL):
            owner = col + N_COL * (place // N_COL)
            pairs.append((place * N_COL + col, owner * N_COL + place % N_COL))
    return pairs


def on_device(parent_sigma, slot_tile, slot_count, panel, sep_factor):
    my_row = lax.axis_index(ROW).astype(jnp.int32)
    my_col = lax.axis_index(COL).astype(jnp.int32)
    me = jnp.stack([my_row, my_col])
    sigma = parent_sigma.reshape(4, TILE * 8, TILE)
    with jax.named_scope("front_product"):
        partial = front(slot_tile, slot_count, me, sigma, panel).reshape(N_ROW, WIDTH, 2 * TILE)
    with jax.named_scope("factor_gather"):
        lines, partial = lax.optimization_barrier((spread_lines(sep_factor, my_col), partial))
        shares = gather_factor(lines)
    with jax.named_scope("front_sum"):
        half = total(exchange(partial.reshape(X, Y, WIDTH, 2 * TILE), "x"))
        piece = total(exchange(half, "y"))
        piece = lax.ppermute(piece, ROW + COL, to_slot_owner())
    with jax.named_scope("front_gather"):
        whole = lax.all_gather(piece, COL, axis=0, tiled=True)
    with jax.named_scope("inverse"):
        shares, _ = lax.optimization_barrier((shares, piece))
        inverse = factor_inverse(shares)
    with jax.named_scope("separator"):
        sent = separator(me, slot_count, piece, panel, inverse)
        taken = total(exchange(sent, ROW))
        blocks = exchange(lax.optimization_barrier(spread(taken, N_COL)), COL)
    with jax.named_scope("final"):
        return final(me, slot_count, whole, blocks, inverse)


def solution(mesh):
    inner = Mesh(np.array(mesh.devices).reshape(X, Y, Z, CORE), ROW + COL)
    placed = (
        P(None, ROW, None, None, COL, None),
        P(),
        P(),
        P(ROW, None, None, None),
        P(ROW, None),
    )
    return jax.shard_map(
        on_device,
        mesh=inner,
        in_specs=placed,
        out_specs=(P(ROW, None, None, None), P(ROW, None)),
        check_vma=False,
    )
```

```python
import functools

import jax
import jax.numpy as jnp
import numpy as np
from jax import lax
from jax.experimental import pallas as pl
from jax.experimental.pallas import tpu as pltpu
from jax.sharding import Mesh
from jax.sharding import PartitionSpec as P

ROW = ("x", "y")
COL = ("z", "core")
X, Y, Z, CORE = 4, 8, 8, 2
N_ROW, N_COL = X * Y, Z * CORE
TILE = 128
SEP = 1024
STRIPE = SEP // X
PACKED = STRIPE * X * (X + 1) // 2
WIDTH = SEP // N_COL
OWN = SEP // N_ROW
LINES = OWN // N_COL
MIB = 1024 * 1024


def split(value):
    high = value.astype(jnp.bfloat16)
    return high, (value - high.astype(jnp.float32)).astype(jnp.bfloat16)


def split_dot(left, right):
    def dot(first, last):
        return jnp.dot(first, last, preferred_element_type=jnp.float32)

    (left_high, left_low), (right_high, right_low) = left, right
    return dot(left_high, right_high) + (dot(left_high, right_low) + dot(left_low, right_high))


def fine_dot(left, right):
    return split_dot(split(left), split(right))


def on_chip(value):
    return pltpu.with_memory_space_constraint(value, pltpu.VMEM)


def off_chip(value):
    return pltpu.with_memory_space_constraint(value, pltpu.HBM)


def front_kernel(tile_ref, count_ref, me_ref, upper_ref, lower_ref, panel_ref, out_ref):
    row, col = me_ref[0], me_ref[1]
    live = [(slot < count_ref[row]).astype(jnp.float32) for slot in range(2)]
    strips = jnp.concatenate([panel_ref[0, slot] * live[slot] for slot in range(2)], axis=0)
    strips_t = strips.T
    for step in range(2):
        owner = col + N_COL * step
        block = jnp.concatenate(
            [
                jnp.concatenate(
                    [sigma[0, pl.ds(tile_ref[owner, slot] * 2 + step, TILE, stride=8), :] for slot in range(2)],
                    axis=1,
                )
                for sigma in (upper_ref, lower_ref)
            ],
            axis=0,
        )
        out_ref[step] = fine_dot(strips_t, block)


def front(slot_tile, slot_count, me, sigma, panel):
    def slab(slot):
        return pl.BlockSpec((1, TILE * 8, TILE), lambda i, tile, count, me: (tile[me[0], slot], 0, 0))

    return pl.pallas_call(
        front_kernel,
        grid_spec=pltpu.PrefetchScalarGridSpec(
            num_scalar_prefetch=3,
            grid=(1,),
            in_specs=[
                slab(0),
                slab(1),
                pl.BlockSpec((1, 2, TILE, SEP), lambda i, *_: (0, 0, 0, 0)),
            ],
            out_specs=pl.BlockSpec((2, SEP, 2 * TILE), lambda i, *_: (0, 0, 0)),
        ),
        out_shape=jax.ShapeDtypeStruct((2, SEP, 2 * TILE), jnp.float32),
        compiler_params=pltpu.CompilerParams(vmem_limit_bytes=16 * MIB),
        name="front",
    )(slot_tile, slot_count, me, off_chip(sigma), off_chip(sigma), off_chip(panel))


def invert_tiles(tiles):
    row = lax.broadcasted_iota(jnp.int32, (TILE, TILE), 0)
    col = lax.broadcasted_iota(jnp.int32, (TILE, TILE), 1)

    def left_of(size):
        return (row // (2 * size) == col // (2 * size)) & (row // size > col // size)

    inverses = []
    for tile in tiles:
        scale = jnp.where(row == col, 1.0 / jnp.where(row == col, tile, 1.0), 0.0)
        down = jnp.sum(scale, axis=1, keepdims=True)
        across = jnp.sum(scale, axis=0, keepdims=True)
        inverses.append(scale - jnp.where(left_of(1), tile * down * across, 0.0))
    size = 2
    while size < TILE:
        mask = left_of(size)
        halves = [split(inverse) for inverse in inverses]
        products = [split_dot(split(jnp.where(mask, tile, 0.0)), half) for tile, half in zip(tiles, halves)]
        inverses = [
            inverse - split_dot(half, split(product)) for inverse, half, product in zip(inverses, halves, products)
        ]
        size *= 2
    return inverses


def inverse_kernel(share_ref, out_ref, packed_ref):
    for block in range(PACKED // TILE):
        for y in range(Y):
            for line in range(LINES):
                start = (block * Y + y) * LINES + line
                taken = share_ref[pl.ds(start, N_COL, stride=PACKED // TILE * Y * LINES), :]
                packed_ref[block, pl.ds(y * OWN + line, N_COL, stride=LINES), :] = taken

    def factor(stripe, start, width):
        first = (STRIPE * stripe * (stripe + 1) // 2 + start) // TILE
        return jnp.concatenate([packed_ref[first + block] for block in range(width // TILE)], axis=1)

    diagonals = [factor(stripe, stripe * STRIPE, STRIPE) for stripe in range(X)]
    tiles = [d[p * TILE : (p + 1) * TILE, p * TILE : (p + 1) * TILE] for d in diagonals for p in range(2)]
    inverses = invert_tiles(tiles)
    middles = [fine_dot(d[TILE:, :TILE], inverses[2 * stripe]) for stripe, d in enumerate(diagonals)]
    corners = [-fine_dot(inverses[2 * stripe + 1], middle) for stripe, middle in enumerate(middles)]
    for stripe in range(X):
        top = stripe * STRIPE
        out_ref[top : top + TILE, top : top + TILE] = inverses[2 * stripe]
        out_ref[top : top + TILE, top + TILE :] = jnp.zeros((TILE, SEP - top - TILE), jnp.float32)
        out_ref[top + TILE : top + STRIPE, top : top + TILE] = corners[stripe]
        out_ref[top + TILE : top + STRIPE, top + TILE : top + STRIPE] = inverses[2 * stripe + 1]
        if stripe < X - 1:
            out_ref[top + TILE : top + STRIPE, top + STRIPE :] = jnp.zeros((TILE, SEP - top - STRIPE), jnp.float32)
    products = []
    for stripe in (1, 3):
        left = (stripe - 1) * STRIPE
        above = out_ref[left : left + STRIPE, left : left + STRIPE]
        products.append(fine_dot(factor(stripe, left, STRIPE), above))
    for stripe, product in zip((1, 3), products):
        top = stripe * STRIPE
        own = out_ref[top : top + STRIPE, top : top + STRIPE]
        out_ref[top : top + STRIPE, top - STRIPE : top] = -fine_dot(own, product)
    half = 2 * STRIPE
    left_part = jnp.concatenate([factor(2, 0, half), factor(3, 0, half)], axis=0)
    first_cols = fine_dot(left_part, out_ref[:half, :STRIPE])
    last_cols = fine_dot(left_part[:, STRIPE:], out_ref[STRIPE:half, STRIPE:half])
    product = jnp.concatenate([first_cols, last_cols], axis=1)
    out_ref[half : half + STRIPE, :half] = -fine_dot(out_ref[half : half + STRIPE, half : half + STRIPE], product[:STRIPE])
    out_ref[half + STRIPE :, :half] = -fine_dot(out_ref[half + STRIPE :, half:], product)


VMEM = pl.BlockSpec(memory_space=pltpu.VMEM)
SMEM = pl.BlockSpec(memory_space=pltpu.SMEM)


def factor_inverse(shares):
    return pl.pallas_call(
        inverse_kernel,
        in_specs=[VMEM],
        out_specs=VMEM,
        out_shape=jax.ShapeDtypeStruct((SEP, SEP), jnp.float32),
        scratch_shapes=[pltpu.VMEM((PACKED // TILE, STRIPE, TILE), jnp.float32)],
        compiler_params=pltpu.CompilerParams(vmem_limit_bytes=20 * MIB),
        name="factor_inverse",
    )(shares)


def times_inverse(left_ref, inverse_ref, stripe):
    start = stripe * STRIPE
    return fine_dot(left_ref[:, start:], inverse_ref[start:, :])


def for_stripe(body):
    for stripe in range(X):
        pl.when(pl.program_id(0) == stripe)(functools.partial(body, stripe))


def whole_block(shape):
    return pl.BlockSpec(shape, lambda i: (0,) * len(shape))


def separator_kernel(me_ref, count_ref, piece_ref, panel_ref, inverse_ref, out_ref):
    row, col = me_ref[0], me_ref[1]
    live = [(slot < count_ref[row]).astype(jnp.float32) for slot in range(2)]
    strips = jnp.concatenate([panel_ref[0, slot] * live[slot] for slot in range(2)], axis=0)
    local = fine_dot(piece_ref[...], strips)
    down = lax.broadcasted_iota(jnp.int32, (WIDTH, SEP), 0) + col * WIDTH
    across = lax.broadcasted_iota(jnp.int32, (WIDTH, SEP), 1)
    local = local + jnp.where((down == across) & (row == 0), 1.0, 0.0)
    for stripe in range(X):
        first = stripe * STRIPE
        turned = fine_dot(local[:, first:], inverse_ref[first:, first : first + STRIPE]).T
        for place in range(STRIPE // OWN):
            start = place * OWN
            out_ref[stripe * (STRIPE // OWN) + place] = jnp.concatenate(
                [turned[start : start + OWN // 2], turned[start + OWN // 2 : start + OWN]], axis=1
            )


def separator(me, slot_count, piece, panel, inverse):
    return pl.pallas_call(
        separator_kernel,
        in_specs=[SMEM, SMEM, VMEM, VMEM, VMEM],
        out_specs=VMEM,
        out_shape=jax.ShapeDtypeStruct((N_ROW, OWN // 2, 2 * WIDTH), jnp.float32),
        compiler_params=pltpu.CompilerParams(vmem_limit_bytes=14 * MIB),
        name="separator",
    )(me, slot_count, piece, panel, inverse)


def update_kernel(me_ref, count_ref, whole_ref, inverse_ref, update_ref, left_ref):
    @pl.when(pl.program_id(0) == 0)
    def _():
        row = me_ref[0]
        turned = whole_ref[...].T
        for slot in range(2):
            sign = -(slot < count_ref[row]).astype(jnp.float32)
            left_ref[slot * TILE : (slot + 1) * TILE, :] = turned[slot * TILE : (slot + 1) * TILE] * sign

    @for_stripe
    def _(stripe):
        result = times_inverse(left_ref, inverse_ref, stripe)
        update_ref[0, 0] = result[:TILE]
        update_ref[0, 1] = result[TILE:]


def update_rows(me, slot_count, whole, inverse):
    return pl.pallas_call(
        update_kernel,
        grid=(X,),
        in_specs=[
            SMEM,
            SMEM,
            whole_block((SEP, 2 * TILE)),
            pl.BlockSpec((SEP, STRIPE), lambda i: (0, i)),
        ],
        out_specs=pl.BlockSpec((1, 2, TILE, STRIPE), lambda i: (0, 0, 0, i)),
        out_shape=jax.ShapeDtypeStruct((1, 2, TILE, SEP), jnp.float32),
        scratch_shapes=[pltpu.VMEM((2 * TILE, SEP), jnp.float32)],
        compiler_params=pltpu.CompilerParams(vmem_limit_bytes=16 * MIB),
        name="update_rows",
    )(me, slot_count, off_chip(whole), off_chip(inverse))


def separator_rows_kernel(blocks_ref, inverse_ref, sep_ref, left_ref):
    @pl.when(pl.program_id(0) == 0)
    def _():
        for side in range(2):
            lanes = slice(side * WIDTH, (side + 1) * WIDTH)
            start = side * (OWN // 2)
            left_ref[start : start + OWN // 2, :] = jnp.concatenate(
                [blocks_ref[place][:, lanes] for place in range(N_COL)], axis=1
            )

    @for_stripe
    def _(stripe):
        sep_ref[...] = times_inverse(left_ref, inverse_ref, stripe)


def separator_rows(blocks, inverse):
    return pl.pallas_call(
        separator_rows_kernel,
        grid=(X,),
        in_specs=[
            whole_block((N_COL, OWN // 2, 2 * WIDTH)),
            pl.BlockSpec((SEP, STRIPE), lambda i: (0, i)),
        ],
        out_specs=pl.BlockSpec((OWN, STRIPE), lambda i: (0, i)),
        out_shape=jax.ShapeDtypeStruct((OWN, SEP), jnp.float32),
        scratch_shapes=[pltpu.VMEM((OWN, SEP), jnp.float32)],
        compiler_params=pltpu.CompilerParams(vmem_limit_bytes=12 * MIB),
        name="separator_rows",
    )(blocks, off_chip(inverse))


def total_kernel(pieces_ref, out_ref):
    out_ref[...] = jnp.sum(pieces_ref[...], axis=0)


def total(pieces):
    return pl.pallas_call(
        total_kernel,
        in_specs=[VMEM],
        out_specs=VMEM,
        out_shape=jax.ShapeDtypeStruct(pieces.shape[1:], jnp.float32),
        compiler_params=pltpu.CompilerParams(vmem_limit_bytes=8 * MIB),
        name="total",
    )(on_chip(pieces))


def spread(value, size):
    return jnp.broadcast_to(value[None], (size, *value.shape))


def exchange(blocks, axis):
    return lax.all_to_all(blocks, axis, 0, 0, tiled=True)


def spread_lines(sep_factor, col):
    return exchange(spread(lax.dynamic_slice_in_dim(sep_factor, col * LINES, LINES, 0), N_ROW), ROW)


def gather_factor(lines):
    stripes = lines.reshape(X, Y * LINES, SEP // TILE, TILE)
    count = STRIPE // TILE
    packed = jnp.concatenate([stripes[i, :, : count * (i + 1)].transpose(1, 0, 2) for i in range(X)], axis=0)
    return lax.all_gather(packed, COL, axis=0, tiled=True).reshape(-1, TILE)


def to_slot_owner():
    pairs = []
    for place in range(N_ROW):
        for col in range(N_COL):
            owner = col + N_COL * (place // N_COL)
            pairs.append((place * N_COL + col, owner * N_COL + place % N_COL))
    return pairs


def on_device(parent_sigma, slot_tile, slot_count, panel, sep_factor):
    my_row = lax.axis_index(ROW).astype(jnp.int32)
    my_col = lax.axis_index(COL).astype(jnp.int32)
    me = jnp.stack([my_row, my_col])
    sigma = parent_sigma.reshape(4, TILE * 8, TILE)
    with jax.named_scope("front_product"):
        partial = front(slot_tile, slot_count, me, sigma, panel).reshape(N_ROW, WIDTH, 2 * TILE)
    with jax.named_scope("factor_gather"):
        lines, partial = lax.optimization_barrier((spread_lines(sep_factor, my_col), partial))
        shares = gather_factor(lines)
    with jax.named_scope("front_sum"):
        half = total(exchange(partial.reshape(X, Y, WIDTH, 2 * TILE), "x"))
        piece = total(exchange(half, "y"))
        piece = lax.ppermute(piece, ROW + COL, to_slot_owner())
    with jax.named_scope("front_gather"):
        whole = lax.all_gather(piece, COL, axis=0, tiled=True)
    with jax.named_scope("inverse"):
        shares, _ = lax.optimization_barrier((shares, piece))
        inverse = factor_inverse(shares)
    with jax.named_scope("separator"):
        sent = separator(me, slot_count, piece, panel, inverse)
        taken = total(exchange(sent, ROW))
        blocks = exchange(lax.optimization_barrier(spread(taken, N_COL)), COL)
    with jax.named_scope("final"):
        return update_rows(me, slot_count, whole, inverse), separator_rows(blocks, inverse)


def solution(mesh):
    inner = Mesh(np.array(mesh.devices).reshape(X, Y, Z, CORE), ROW + COL)
    placed = (
        P(None, ROW, None, None, COL, None),
        P(),
        P(),
        P(ROW, None, None, None),
        P(ROW, None),
    )
    return jax.shard_map(
        on_device,
        mesh=inner,
        in_specs=placed,
        out_specs=(P(ROW, None, None, None), P(ROW, None)),
        check_vma=False,
    )
```

```python
import functools

import jax
import jax.numpy as jnp
import numpy as np
from jax import lax
from jax.experimental import pallas as pl
from jax.experimental.pallas import tpu as pltpu
from jax.sharding import Mesh
from jax.sharding import PartitionSpec as P

ROW = ("x", "y")
COL = ("z", "core")
X, Y, Z, CORE = 4, 8, 8, 2
N_ROW, N_COL = X * Y, Z * CORE
TILE = 128
SEP = 1024
STRIPE = SEP // X
PACKED = STRIPE * X * (X + 1) // 2
WIDTH = SEP // N_COL
OWN = SEP // N_ROW
LINES = OWN // N_COL
MIB = 1024 * 1024


def split(value):
    high = value.astype(jnp.bfloat16)
    return high, (value - high.astype(jnp.float32)).astype(jnp.bfloat16)


def split_dot(left, right):
    def dot(first, last):
        return jnp.dot(first, last, preferred_element_type=jnp.float32)

    (left_high, left_low), (right_high, right_low) = left, right
    return dot(left_high, right_high) + (dot(left_high, right_low) + dot(left_low, right_high))


def fine_dot(left, right):
    return split_dot(split(left), split(right))


def on_chip(value):
    return pltpu.with_memory_space_constraint(value, pltpu.VMEM)


def off_chip(value):
    return pltpu.with_memory_space_constraint(value, pltpu.HBM)


def front_kernel(tile_ref, count_ref, me_ref, upper_ref, lower_ref, panel_ref, out_ref):
    row, col = me_ref[0], me_ref[1]
    live = [(slot < count_ref[row]).astype(jnp.float32) for slot in range(2)]
    strips = jnp.concatenate([panel_ref[0, slot] * live[slot] for slot in range(2)], axis=0)
    strips_t = strips.T
    for step in range(2):
        owner = col + N_COL * step
        block = jnp.concatenate(
            [
                jnp.concatenate(
                    [sigma[0, pl.ds(tile_ref[owner, slot] * 2 + step, TILE, stride=8), :] for slot in range(2)],
                    axis=1,
                )
                for sigma in (upper_ref, lower_ref)
            ],
            axis=0,
        )
        out_ref[step] = fine_dot(strips_t, block)


def front(slot_tile, slot_count, me, sigma, panel):
    def slab(slot):
        return pl.BlockSpec((1, TILE * 8, TILE), lambda i, tile, count, me: (tile[me[0], slot], 0, 0))

    return pl.pallas_call(
        front_kernel,
        grid_spec=pltpu.PrefetchScalarGridSpec(
            num_scalar_prefetch=3,
            grid=(1,),
            in_specs=[
                slab(0),
                slab(1),
                pl.BlockSpec((1, 2, TILE, SEP), lambda i, *_: (0, 0, 0, 0)),
            ],
            out_specs=pl.BlockSpec((2, SEP, 2 * TILE), lambda i, *_: (0, 0, 0)),
        ),
        out_shape=jax.ShapeDtypeStruct((2, SEP, 2 * TILE), jnp.float32),
        compiler_params=pltpu.CompilerParams(vmem_limit_bytes=16 * MIB),
        name="front",
    )(slot_tile, slot_count, me, off_chip(sigma), off_chip(sigma), off_chip(panel))


def invert_tiles(tiles):
    row = lax.broadcasted_iota(jnp.int32, (TILE, TILE), 0)
    col = lax.broadcasted_iota(jnp.int32, (TILE, TILE), 1)

    def left_of(size):
        return (row // (2 * size) == col // (2 * size)) & (row // size > col // size)

    inverses = []
    for tile in tiles:
        scale = jnp.where(row == col, 1.0 / jnp.where(row == col, tile, 1.0), 0.0)
        down = jnp.sum(scale, axis=1, keepdims=True)
        across = jnp.sum(scale, axis=0, keepdims=True)
        inverses.append(scale - jnp.where(left_of(1), tile * down * across, 0.0))
    size = 2
    while size < TILE:
        mask = left_of(size)
        halves = [split(inverse) for inverse in inverses]
        products = [split_dot(split(jnp.where(mask, tile, 0.0)), half) for tile, half in zip(tiles, halves)]
        inverses = [
            inverse - split_dot(half, split(product)) for inverse, half, product in zip(inverses, halves, products)
        ]
        size *= 2
    return inverses


def inverse_kernel(share_ref, out_ref, packed_ref):
    for block in range(PACKED // TILE):
        for y in range(Y):
            for line in range(LINES):
                start = (block * Y + y) * LINES + line
                taken = share_ref[pl.ds(start, N_COL, stride=PACKED // TILE * Y * LINES), :]
                packed_ref[block, pl.ds(y * OWN + line, N_COL, stride=LINES), :] = taken

    def factor(stripe, start, width):
        first = (STRIPE * stripe * (stripe + 1) // 2 + start) // TILE
        return jnp.concatenate([packed_ref[first + block] for block in range(width // TILE)], axis=1)

    diagonals = [factor(stripe, stripe * STRIPE, STRIPE) for stripe in range(X)]
    tiles = [d[p * TILE : (p + 1) * TILE, p * TILE : (p + 1) * TILE] for d in diagonals for p in range(2)]
    inverses = invert_tiles(tiles)
    middles = [fine_dot(d[TILE:, :TILE], inverses[2 * stripe]) for stripe, d in enumerate(diagonals)]
    corners = [-fine_dot(inverses[2 * stripe + 1], middle) for stripe, middle in enumerate(middles)]
    for stripe in range(X):
        top = stripe * STRIPE
        out_ref[top : top + TILE, top : top + TILE] = inverses[2 * stripe]
        out_ref[top : top + TILE, top + TILE :] = jnp.zeros((TILE, SEP - top - TILE), jnp.float32)
        out_ref[top + TILE : top + STRIPE, top : top + TILE] = corners[stripe]
        out_ref[top + TILE : top + STRIPE, top + TILE : top + STRIPE] = inverses[2 * stripe + 1]
        if stripe < X - 1:
            out_ref[top + TILE : top + STRIPE, top + STRIPE :] = jnp.zeros((TILE, SEP - top - STRIPE), jnp.float32)
    products = []
    for stripe in (1, 3):
        left = (stripe - 1) * STRIPE
        above = out_ref[left : left + STRIPE, left : left + STRIPE]
        products.append(fine_dot(factor(stripe, left, STRIPE), above))
    for stripe, product in zip((1, 3), products):
        top = stripe * STRIPE
        own = out_ref[top : top + STRIPE, top : top + STRIPE]
        out_ref[top : top + STRIPE, top - STRIPE : top] = -fine_dot(own, product)
    half = 2 * STRIPE
    left_part = jnp.concatenate([factor(2, 0, half), factor(3, 0, half)], axis=0)
    first_cols = fine_dot(left_part, out_ref[:half, :STRIPE])
    last_cols = fine_dot(left_part[:, STRIPE:], out_ref[STRIPE:half, STRIPE:half])
    product = jnp.concatenate([first_cols, last_cols], axis=1)
    out_ref[half : half + STRIPE, :half] = -fine_dot(out_ref[half : half + STRIPE, half : half + STRIPE], product[:STRIPE])
    out_ref[half + STRIPE :, :half] = -fine_dot(out_ref[half + STRIPE :, half:], product)


VMEM = pl.BlockSpec(memory_space=pltpu.VMEM)
SMEM = pl.BlockSpec(memory_space=pltpu.SMEM)


def factor_inverse(shares):
    return pl.pallas_call(
        inverse_kernel,
        in_specs=[VMEM],
        out_specs=VMEM,
        out_shape=jax.ShapeDtypeStruct((SEP, SEP), jnp.float32),
        scratch_shapes=[pltpu.VMEM((PACKED // TILE, STRIPE, TILE), jnp.float32)],
        compiler_params=pltpu.CompilerParams(vmem_limit_bytes=20 * MIB),
        name="factor_inverse",
    )(shares)


def times_inverse(left_ref, inverse_ref, stripe):
    start = stripe * STRIPE
    return fine_dot(left_ref[:, start:], inverse_ref[start:, :])


def for_stripe(body):
    for stripe in range(X):
        pl.when(pl.program_id(0) == stripe)(functools.partial(body, stripe))


def whole_block(shape):
    return pl.BlockSpec(shape, lambda i: (0,) * len(shape))


def separator_kernel(me_ref, count_ref, piece_ref, panel_ref, inverse_ref, out_ref):
    row, col = me_ref[0], me_ref[1]
    live = [(slot < count_ref[row]).astype(jnp.float32) for slot in range(2)]
    strips = jnp.concatenate([panel_ref[0, slot] * live[slot] for slot in range(2)], axis=0)
    local = fine_dot(piece_ref[...], strips)
    down = lax.broadcasted_iota(jnp.int32, (WIDTH, SEP), 0) + col * WIDTH
    across = lax.broadcasted_iota(jnp.int32, (WIDTH, SEP), 1)
    local = local + jnp.where((down == across) & (row == 0), 1.0, 0.0)
    for stripe in range(X):
        first = stripe * STRIPE
        turned = fine_dot(local[:, first:], inverse_ref[first:, first : first + STRIPE]).T
        for place in range(STRIPE // OWN):
            start = place * OWN
            out_ref[stripe * (STRIPE // OWN) + place] = jnp.concatenate(
                [turned[start : start + OWN // 2], turned[start + OWN // 2 : start + OWN]], axis=1
            )


def separator(me, slot_count, piece, panel, inverse):
    return pl.pallas_call(
        separator_kernel,
        in_specs=[SMEM, SMEM, VMEM, VMEM, VMEM],
        out_specs=VMEM,
        out_shape=jax.ShapeDtypeStruct((N_ROW, OWN // 2, 2 * WIDTH), jnp.float32),
        compiler_params=pltpu.CompilerParams(vmem_limit_bytes=14 * MIB),
        name="separator",
    )(me, slot_count, piece, panel, inverse)


def update_kernel(me_ref, count_ref, whole_ref, inverse_ref, update_ref, left_ref):
    @pl.when(pl.program_id(0) == 0)
    def _():
        row = me_ref[0]
        turned = whole_ref[...].T
        for slot in range(2):
            sign = -(slot < count_ref[row]).astype(jnp.float32)
            left_ref[slot * TILE : (slot + 1) * TILE, :] = turned[slot * TILE : (slot + 1) * TILE] * sign

    @for_stripe
    def _(stripe):
        result = times_inverse(left_ref, inverse_ref, stripe)
        update_ref[0, 0] = result[:TILE]
        update_ref[0, 1] = result[TILE:]


def update_rows(me, slot_count, whole, inverse):
    return pl.pallas_call(
        update_kernel,
        grid=(X,),
        in_specs=[
            SMEM,
            SMEM,
            whole_block((SEP, 2 * TILE)),
            pl.BlockSpec((SEP, STRIPE), lambda i: (0, i)),
        ],
        out_specs=pl.BlockSpec((1, 2, TILE, STRIPE), lambda i: (0, 0, 0, i)),
        out_shape=jax.ShapeDtypeStruct((1, 2, TILE, SEP), jnp.float32),
        scratch_shapes=[pltpu.VMEM((2 * TILE, SEP), jnp.float32)],
        compiler_params=pltpu.CompilerParams(vmem_limit_bytes=16 * MIB),
        name="update_rows",
    )(me, slot_count, off_chip(whole), off_chip(inverse))


def separator_rows_kernel(blocks_ref, inverse_ref, sep_ref, held_ref, arrived):
    def rows(stripe):
        return pl.ds(stripe * STRIPE, STRIPE), pl.ds(0, (stripe + 1) * STRIPE)

    copies = [
        pltpu.make_async_copy(inverse_ref.at[rows(stripe)], held_ref.at[rows(stripe)], arrived.at[stripe])
        for stripe in range(X)
    ]
    for copy in reversed(copies):
        copy.start()
    blocks = [blocks_ref[place] for place in range(N_COL)]
    sides = [
        jnp.concatenate([block[:, side * WIDTH : (side + 1) * WIDTH] for block in blocks], axis=1) for side in range(2)
    ]
    left = jnp.concatenate(sides, axis=0)
    for stripe in reversed(range(X)):
        copies[stripe].wait()
        first = stripe * STRIPE
        lanes = slice(first, first + STRIPE)
        sep_ref[:, lanes] = fine_dot(left[:, first:], held_ref[first:, lanes])


def separator_rows(blocks, inverse):
    return pl.pallas_call(
        separator_rows_kernel,
        in_specs=[VMEM, pl.BlockSpec(memory_space=pl.ANY)],
        out_specs=VMEM,
        out_shape=jax.ShapeDtypeStruct((OWN, SEP), jnp.float32),
        scratch_shapes=[pltpu.VMEM((SEP, SEP), jnp.float32), pltpu.SemaphoreType.DMA((X,))],
        compiler_params=pltpu.CompilerParams(vmem_limit_bytes=12 * MIB),
        name="separator_rows",
    )(blocks, off_chip(inverse))


def total_kernel(pieces_ref, out_ref):
    out_ref[...] = jnp.sum(pieces_ref[...], axis=0)


def total(pieces):
    return pl.pallas_call(
        total_kernel,
        in_specs=[VMEM],
        out_specs=VMEM,
        out_shape=jax.ShapeDtypeStruct(pieces.shape[1:], jnp.float32),
        compiler_params=pltpu.CompilerParams(vmem_limit_bytes=8 * MIB),
        name="total",
    )(on_chip(pieces))


def spread(value, size):
    return jnp.broadcast_to(value[None], (size, *value.shape))


def exchange(blocks, axis):
    return lax.all_to_all(blocks, axis, 0, 0, tiled=True)


def spread_lines(sep_factor, col):
    return exchange(spread(lax.dynamic_slice_in_dim(sep_factor, col * LINES, LINES, 0), N_ROW), ROW)


def gather_factor(lines):
    stripes = lines.reshape(X, Y * LINES, SEP // TILE, TILE)
    count = STRIPE // TILE
    packed = jnp.concatenate([stripes[i, :, : count * (i + 1)].transpose(1, 0, 2) for i in range(X)], axis=0)
    return lax.all_gather(packed, COL, axis=0, tiled=True).reshape(-1, TILE)


def to_slot_owner():
    pairs = []
    for place in range(N_ROW):
        for col in range(N_COL):
            owner = col + N_COL * (place // N_COL)
            pairs.append((place * N_COL + col, owner * N_COL + place % N_COL))
    return pairs


def on_device(parent_sigma, slot_tile, slot_count, panel, sep_factor):
    my_row = lax.axis_index(ROW).astype(jnp.int32)
    my_col = lax.axis_index(COL).astype(jnp.int32)
    me = jnp.stack([my_row, my_col])
    sigma = parent_sigma.reshape(4, TILE * 8, TILE)
    with jax.named_scope("front_product"):
        partial = front(slot_tile, slot_count, me, sigma, panel).reshape(N_ROW, WIDTH, 2 * TILE)
    with jax.named_scope("factor_gather"):
        lines, partial = lax.optimization_barrier((spread_lines(sep_factor, my_col), partial))
        shares = gather_factor(lines)
    with jax.named_scope("front_sum"):
        half = total(exchange(partial.reshape(X, Y, WIDTH, 2 * TILE), "x"))
        piece = total(exchange(half, "y"))
        piece = lax.ppermute(piece, ROW + COL, to_slot_owner())
    with jax.named_scope("front_gather"):
        whole = lax.all_gather(piece, COL, axis=0, tiled=True)
    with jax.named_scope("inverse"):
        shares, _ = lax.optimization_barrier((shares, piece))
        inverse = factor_inverse(shares)
    with jax.named_scope("separator"):
        sent = separator(me, slot_count, piece, panel, inverse)
        taken = total(exchange(sent, ROW))
        blocks = exchange(lax.optimization_barrier(spread(taken, N_COL)), COL)
    with jax.named_scope("final"):
        return update_rows(me, slot_count, whole, inverse), separator_rows(blocks, inverse)


def solution(mesh):
    inner = Mesh(np.array(mesh.devices).reshape(X, Y, Z, CORE), ROW + COL)
    placed = (
        P(None, ROW, None, None, COL, None),
        P(),
        P(),
        P(ROW, None, None, None),
        P(ROW, None),
    )
    return jax.shard_map(
        on_device,
        mesh=inner,
        in_specs=placed,
        out_specs=(P(ROW, None, None, None), P(ROW, None)),
        check_vma=False,
    )
```
